32 devices in a mesh: groups: 2 (over x), role: 2 (over core), seq: 8 (over z, y).
Axes of the slice: x: 2, y: 2, z: 4, core: 2. Of those that a mesh axis runs over, the one named last changes fastest.
Arguments:
- kv_store: bfloat16 [2, 8192, 1024], P('role', ('groups', 'seq')), parts along dimension 1, may hold values from -6 to 6
- queries: bfloat16 [2, 256, 2, 4096], P('role', ('groups', 'seq')), parts along dimension 1, may hold values from -100 to 100
- step_kv: bfloat16 [256, 2, 1024], P(('groups', 'seq')), parts along dimension 0, may hold values from -6 to 6
- suffix_pages: int32 [256, 2], P(('groups', 'seq')), parts along dimension 0, may hold values from 0 to 31, as said below
- suffix_len: int32 [256], P(('groups', 'seq')), parts along dimension 0, may hold values from 2 to 32, as said below
- owner: int32 [256, 1], P(('groups', 'seq')), parts along dimension 0, may hold values from 0 to 7; in each aligned block of 16 rows (0 to 15, 16 to 31, ...) at most 4 rows name the same one
- parent_id: int32 [256], P(('groups', 'seq')), parts along dimension 0, may hold values from 0 to 1
- parent_pages: int32 [32, 16], P(('groups', 'seq')), parts along dimension 0, may hold values from 0 to 31, as said below
- parent_len: int32 [32], P(('groups', 'seq')), parts along dimension 0, may hold values from 1 to 256, as said below
Outputs:
- served: bfloat16 [2, 256, 2, 4096], P('role', ('groups', 'seq')), parts along dimension 1
The draws below stay inside these ranges and needn't reach their ends.
There are 2 independent parts, one for each index of `groups`. The reference program is written for one: setup_inputs(seed, part) draws one part's arguments, and reference() takes and returns one part's arrays. A program takes and returns all parts, laid end to end along the dimension named above; each array names one. Nothing has to cross between parts.
Inputs may be any that keep to these rules, and one draw needn't show every extreme that they name: `suffix_pages`: on each device the page lists of its 16 requests are disjoint and together name every page of its store once. `suffix_len`: the first request of every device has the full 32 tokens. Of the requests of one device at most 4 go to one owner, and some device sends 4 to one owner. `parent_pages`: on each device the page tables of its 2 parent slots are disjoint and together name every page of its store once. `parent_len`: the first parent slot of every device has the full 256 tokens.
All inputs are finite; a program needn't handle non-finite values.
Results may differ from the reference program's by a relative error of at most 0.0025.
Values may be sent and summed in bfloat16 or wider, within the bound.
A program may use at most 128 MiB of HBM per device.

```python
import math
import jax
import jax.numpy as jnp
import numpy as np
from jax import lax

HEAD_DIM = 128
KV_HEADS = 4
GROUP = 8
PAGE = 16
SUF_PAGES = 2
REQ_DEV = 16
PARENTS = 2
QW = 4096
KVW = 1024
SUF = 32
STORE_PAGES = 32
PAR_PAGES = 16
PCTX = 256
CAP = 4
REQUESTS = 128
PAR_ALL = 16
N_SEQ = 8


def shared_draws(key):
    key_store = jax.random.fold_in(key, 101)
    key_query = jax.random.fold_in(key, 102)
    key_step = jax.random.fold_in(key, 103)
    key_pages = jax.random.fold_in(key, 104)
    devices = REQUESTS // REQ_DEV
    page_store = jnp.clip(jax.random.normal(key_store, (2, devices * STORE_PAGES * PAGE, KVW), jnp.float32), -6.0, 6.0)
    query_rows = jnp.clip(2.5 * jax.random.normal(key_query, (2, REQUESTS, 2, QW), jnp.float32), -15.0, 15.0)
    step_rows = jnp.clip(jax.random.normal(key_step, (REQUESTS, 2, KVW), jnp.float32), -6.0, 6.0)
    page_keys = jax.random.split(key_pages, devices)
    page_lists = jax.vmap(lambda subkey: jax.random.permutation(subkey, STORE_PAGES))(page_keys)
    page_lists = page_lists.reshape(REQUESTS, SUF_PAGES).astype(jnp.int32)
    return (page_store, query_rows, step_rows, page_lists)


def draw_kv_store(key, part):
    return shared_draws(key)[0].astype(jnp.bfloat16)


def draw_queries(key, part):
    return shared_draws(key)[1].astype(jnp.bfloat16)


def draw_step_kv(key, part):
    return shared_draws(key)[2].astype(jnp.bfloat16)


def draw_suffix_pages(key, part):
    return shared_draws(key)[3]


def draw_suffix_len(key, part):
    lengths = jax.random.randint(jax.random.fold_in(key, 201), (REQUESTS,), 2, SUF + 1, jnp.int32)
    return lengths.at[::REQ_DEV].set(SUF)


def draw_parent_pages(key, part):
    devices = REQUESTS // REQ_DEV
    page_keys = jax.random.split(jax.random.fold_in(key, 202), devices)
    page_lists = jax.vmap(lambda subkey: jax.random.permutation(subkey, STORE_PAGES))(page_keys)
    return page_lists.reshape(devices * PARENTS, PAR_PAGES).astype(jnp.int32)


def draw_parent_len(key, part):
    lengths = jax.random.randint(jax.random.fold_in(key, 203), (PAR_ALL,), 1, PCTX + 1, jnp.int32)
    return lengths.at[::PARENTS].set(PCTX)


def plant(values, stream_key, least, top_value):
    place = [jax.random.randint(jax.random.fold_in(stream_key, axis), (), 0, length) for axis, length in enumerate(values.shape)]
    longest = values.shape.index(max(values.shape))
    beside = place[:longest] + [(place[longest] + 1) % values.shape[longest]] + place[longest + 1:]
    return values.at[tuple(place)].set(least).at[tuple(beside)].set(top_value)


def routed_block(key, own, number, rows, number_of, top, reach, slope):
    sequence = jax.random.permutation(key, number_of)
    heavy_load, common = portions_of(number_of, rows * top, reach, slope, True), portions_of(number_of, rows * top, reach, slope, False)
    places = jnp.arange(number_of)

    def named(tallies, offset_by):
        used = int((tallies > 0).sum())
        fixed = max(1, used // 4)
        moved = fixed + (places - fixed + offset_by * (used - fixed)) % max(1, number_of - fixed)
        return jnp.zeros((number_of,), jnp.int32).at[sequence[jnp.where(places < fixed, places, moved)]].set(jnp.asarray(tallies, jnp.int32))

    tallies = jnp.where(number % 4 == 0, named(heavy_load, number // 4), named(common, number - number // 4 - 1))
    mixed = jax.random.permutation(jax.random.fold_in(own, 3), number_of)
    source_of, taker = mixed[0:number_of // 2 * 2:2], mixed[1:number_of // 2 * 2:2]
    room = jnp.minimum(tallies[source_of] - 1, reach - tallies[taker]) // 2
    room = jnp.where((source_of == sequence[0]) | (taker == sequence[0]) | (tallies[taker] == 0), 0, jnp.maximum(room, 0))
    moved = jax.random.randint(jax.random.fold_in(own, 4), (number_of // 2,), 0, 1 << 20) % (room + 1)
    tallies = tallies.at[source_of].add(-moved).at[taker].add(moved)
    members = jnp.searchsorted(jnp.cumsum(tallies), jnp.arange(rows * top), side="right").astype(jnp.int32)
    table = members.reshape(top, rows).T
    table = table[jax.random.permutation(jax.random.fold_in(own, 1), rows)]
    offset_by = jax.random.randint(jax.random.fold_in(own, 2), (rows, 1), 0, top)
    return jnp.take_along_axis(table, (jnp.arange(top)[None, :] + offset_by) % top, axis=1)


def portions_of(number_of, total, most, skew, full):
    portions = [(1 << 20) // math.isqrt(grade ** skew) + 1 for grade in range(1, number_of + 1)]
    largest = most if full else min(most, max(-(-total // number_of), total * portions[0] // sum(portions)))
    least = 1 if total - largest >= number_of - 1 else 0
    given, surplus = [largest] + [least] * (number_of - 1), total - largest - least * (number_of - 1)
    while surplus > 0:
        free = [i for i in range(1, number_of) if given[i] < largest] or [i for i in range(1, number_of) if given[i] < most]
        pool, budget = sum([portions[i] for i in free]), surplus
        for i in free:
            more = min(most - given[i], max(1, budget * portions[i] // pool), surplus)
            given[i] = given[i] + more
            surplus = surplus - more
    return np.array(given)


def setup_inputs(seed: int = 0, part: int = 0) -> dict:
    key_of = jax.random.split(jax.random.key(seed), 10)
    own_keys = jax.random.split(jax.random.fold_in(key_of[9], part), 10)
    kv_store = draw_kv_store(jax.random.fold_in(jax.random.fold_in(key_of[9], part), 71), part)
    queries = draw_queries(jax.random.fold_in(jax.random.fold_in(key_of[9], part), 71), part)
    step_kv = draw_step_kv(jax.random.fold_in(jax.random.fold_in(key_of[9], part), 71), part)
    suffix_pages = draw_suffix_pages(jax.random.fold_in(jax.random.fold_in(key_of[9], part), 71), part)
    suffix_len = draw_suffix_len(jax.random.fold_in(jax.random.fold_in(key_of[9], part), 71), part)
    owner_keys = jax.random.split(jax.random.fold_in(own_keys[5], 1), REQUESTS // REQ_DEV)
    owner_turns = jax.random.permutation(jax.random.fold_in(own_keys[5], 3), REQUESTS // REQ_DEV)
    owner = jax.vmap(lambda own, number: routed_block(jax.random.fold_in(own_keys[5], 2), own, number, REQ_DEV, N_SEQ, 1, CAP, 2))(owner_keys, owner_turns).reshape((REQUESTS, 1))
    parent_id = plant(jax.random.randint(own_keys[6], (REQUESTS,), 0, PARENTS), jax.random.fold_in(own_keys[6], 1), 0, PARENTS - 1).astype(jnp.int32)
    parent_pages = draw_parent_pages(jax.random.fold_in(jax.random.fold_in(key_of[9], part), 71), part)
    parent_len = draw_parent_len(jax.random.fold_in(jax.random.fold_in(key_of[9], part), 71), part)
    return dict(kv_store=kv_store, queries=queries, step_kv=step_kv, suffix_pages=suffix_pages, suffix_len=suffix_len, owner=owner, parent_id=parent_id, parent_pages=parent_pages, parent_len=parent_len)


MASKED_SCORE = -1e30


def heads_of(kv_rows):
    key_width = KV_HEADS * HEAD_DIM
    shape_head = kv_rows.shape[:-1] + (KV_HEADS, HEAD_DIM)
    return kv_rows[..., :key_width].reshape(shape_head), kv_rows[..., key_width:].reshape(shape_head)


def attend(query_rows, kv_rows, keep_mask):
    request_count = query_rows.shape[0]
    query_heads = query_rows.astype(jnp.float32).reshape(request_count, 2, KV_HEADS, GROUP, HEAD_DIM)
    key_rows, value_rows = heads_of(kv_rows.astype(jnp.float32))
    scores = jnp.einsum("rtgqh,rugh->rtgqu", query_heads, key_rows, precision=lax.Precision.HIGHEST) * HEAD_DIM ** -0.5
    scores = jnp.where(keep_mask[:, :, None, None, :], scores, MASKED_SCORE)
    row_max = jnp.max(scores, axis=-1, keepdims=True)
    exp_terms = jnp.exp(scores - row_max)
    row_total = jnp.sum(exp_terms, axis=-1)
    weights = lax.optimization_barrier(exp_terms.astype(jnp.bfloat16)).astype(jnp.float32)
    blended = jnp.einsum("rtgqu,rugh->rtgqh", weights, value_rows, precision=lax.Precision.HIGHEST)
    blended = blended / row_total[..., None]
    return blended.reshape(request_count, 2, -1).astype(jnp.bfloat16)


def reference(kv_store, queries, step_kv, suffix_pages, suffix_len, owner, parent_id, parent_pages, parent_len):
    page_span = PAGE * KVW
    fresh_store = kv_store[0].reshape(N_SEQ, STORE_PAGES, page_span)
    parent_store = kv_store[1].reshape(N_SEQ, STORE_PAGES, page_span)
    device = (jnp.arange(REQUESTS, dtype=jnp.int32) // REQ_DEV).astype(jnp.int32)
    suffix = fresh_store[device[:, None], suffix_pages].reshape(REQUESTS, SUF, KVW)
    positions = jnp.arange(SUF, dtype=jnp.int32)
    last_seen = suffix_len[:, None] - 2 + jnp.arange(2, dtype=jnp.int32)[None, :]
    keep_prefill = positions[None, None, :] <= last_seen[:, :, None]
    prefilled = attend(queries[0], suffix, keep_prefill)

    def one_device(device_index):
        first_row = (device_index * REQ_DEV).astype(jnp.int32)

        def take_rows(array):
            return lax.dynamic_slice_in_dim(array, first_row, REQ_DEV, 0)

        owner_seq = take_rows(owner)[:, 0]
        parent_slot = owner_seq * PARENTS + take_rows(parent_id)
        page_table = parent_pages[parent_slot]
        context = parent_store[owner_seq[:, None], page_table].reshape(REQ_DEV, PCTX, KVW)
        key_rows = jnp.concatenate([context, take_rows(suffix), take_rows(step_kv)], axis=1)
        keep_parent = jnp.arange(PCTX, dtype=jnp.int32)[None, :] < parent_len[parent_slot][:, None]
        keep_suffix = positions[None, :] < take_rows(suffix_len)[:, None]
        keep_step = jnp.arange(2, dtype=jnp.int32)[None, :] <= jnp.arange(2, dtype=jnp.int32)[:, None]
        keep_mask = jnp.concatenate([
            jnp.broadcast_to(keep_parent[:, None, :], (REQ_DEV, 2, PCTX)),
            jnp.broadcast_to(keep_suffix[:, None, :], (REQ_DEV, 2, SUF)),
            jnp.broadcast_to(keep_step[None, :, :], (REQ_DEV, 2, 2))], axis=2)
        return attend(take_rows(queries[1]), key_rows, keep_mask)

    decoded = lax.map(one_device, jnp.arange(N_SEQ, dtype=jnp.int32)).reshape(REQUESTS, 2, QW)
    return jnp.stack([prefilled, decoded])
```

```python
import functools

import jax
import jax.numpy as jnp
from jax import lax
from jax.experimental import pallas as pl
from jax.experimental.pallas import tpu as pltpu
from jax.sharding import PartitionSpec as P

HEAD_DIM = 128
KV_HEADS = 4
GROUP = 8
PAGE = 16
LANES = 128

MASKED_SCORE = -1e30
MESH = pl.DeviceIdType.MESH


def iota(shape, dim):
    return lax.broadcasted_iota(jnp.int32, shape, dim)


def spread(index, scalars):
    out = jnp.zeros(index.shape, jnp.int32)
    for i, scalar in enumerate(scalars):
        out = jnp.where(index == i, scalar, out)
    return out


def kernel(
    n_seq,
    cap,
    owner_hbm,
    parent_id_hbm,
    suffix_len_hbm,
    suffix_pages_hbm,
    parent_pages_hbm,
    parent_len_hbm,
    q_hbm,
    kv_hbm,
    step_hbm,
    out_ref,
    owner,
    parent_id,
    suffix_len,
    suffix_pages,
    parent_pages,
    parent_len,
    q_ref,
    kv_ref,
    step_in,
    step_ref,
    slots,
    arrived,
    key_meta,
    slot_bias,
    slot_stat,
    far_out,
    near_send,
    near_stat_send,
    ret_send,
    ret,
    partner_q,
    partner_o,
    partner_stat,
    load_sem,
    send_sem,
    recv_sem,
    orecv_sem,
    psend_sem,
    precv_sem,
):
    role = lax.axis_index("role")
    me = lax.axis_index("seq")
    requests, turns, q_width = q_ref.shape
    tokens = requests * turns
    per_peer = 2 * cap
    slot_rows = n_seq * per_peer
    key_count = kv_ref.shape[0]
    key_width = KV_HEADS * HEAD_DIM
    scale = HEAD_DIM ** (-0.5)
    partner = {"role": 1 - role}
    on_decode = role == 1
    on_prefill = role == 0
    heads_all = KV_HEADS * GROUP
    group_width = GROUP * HEAD_DIM
    half = LANES // 2
    unit = min(4, n_seq)
    bits = [(me // 2**b) % 2 for b in range(n_seq.bit_length() - 1)]

    def peer_at(step):
        peer = me
        for b, mine in enumerate(bits):
            if isinstance(step, int):
                if (step >> b) & 1:
                    peer = peer + 2**b * (1 - 2 * mine)
            else:
                peer = peer + 2**b * (1 - 2 * mine) * ((step // 2**b) % 2)
        return peer

    def each(first, last, action):
        def body(i, carry):
            action(i)
            return carry

        lax.fori_loop(first, last, body, 0)

    barrier = pltpu.get_barrier_semaphore()

    def greet(peer):
        pl.semaphore_signal(barrier, inc=1, device_id={"seq": peer}, device_id_type=MESH)

    pl.semaphore_signal(barrier, inc=1, device_id=partner, device_id_type=MESH)

    @pl.when(on_decode)
    def _():
        for step in range(n_seq - 1, 0, -1):
            greet(peer_at(step))

    tables = [
        pltpu.make_async_copy(src, dst, load_sem.at[i])
        for i, (src, dst) in enumerate(
            (
                (owner_hbm, owner),
                (parent_id_hbm, parent_id),
                (suffix_len_hbm, suffix_len),
                (suffix_pages_hbm, suffix_pages),
                (parent_pages_hbm, parent_pages),
                (parent_len_hbm, parent_len),
            )
        )
    ]
    load_step = pltpu.make_async_copy(step_hbm, step_in, load_sem.at[6])
    load_kv = pltpu.make_async_copy(kv_hbm, kv_ref, load_sem.at[7])

    def out_lanes(g):
        return slice(g * group_width, (g + 1) * group_width)

    load_q = [
        pltpu.make_async_copy(
            q_hbm.at[:, :, out_lanes(g)], q_ref.at[:, :, out_lanes(g)], load_sem.at[8 + g]
        )
        for g in range(KV_HEADS)
    ]
    for table in tables[:2]:
        table.start()
    for part in load_q:
        part.start()
    for table in tables[2:]:
        table.start()
    load_kv.start()
    load_step.start()

    def remote(src, dst, ssem, rsem, device):
        return pltpu.make_async_remote_copy(
            src_ref=src,
            dst_ref=dst,
            send_sem=ssem,
            recv_sem=rsem,
            device_id=device,
            device_id_type=MESH,
        )

    q_to_partner = remote(q_ref, partner_q, psend_sem.at[0], precv_sem.at[0], partner)
    o_to_partner = remote(near_send, partner_o, psend_sem.at[1], precv_sem.at[1], partner)
    s_to_partner = remote(near_stat_send, partner_stat, psend_sem.at[2], precv_sem.at[2], partner)

    def q_lanes(g):
        first = 0 if g == 0 else LANES + g * group_width
        return slice(first, LANES + (g + 1) * group_width)

    def ret_lanes(g):
        last = LANES if g == KV_HEADS - 1 else 0
        return slice(g * group_width, (g + 1) * group_width + last)

    def slots_to(step, g):
        peer = peer_at(step)
        return remote(
            slots.at[peer, :, q_lanes(g)],
            arrived.at[me, :, q_lanes(g)],
            send_sem.at[0],
            recv_sem.at[step // unit, g],
            {"seq": peer},
        )

    def slots_from(u, g, count):
        rows = pl.ds(0, count)
        return remote(
            slots.at[rows, :, q_lanes(g)],
            arrived.at[rows, :, q_lanes(g)],
            send_sem.at[0],
            recv_sem.at[u, g],
            {"seq": me},
        )

    def out_to(peer, g):
        return remote(
            ret_send.at[peer, :, ret_lanes(g)],
            ret.at[me, :, ret_lanes(g)],
            send_sem.at[1],
            orecv_sem.at[g],
            {"seq": peer},
        )

    def out_from(g):
        rows = pl.ds(0, n_seq - 1)
        return remote(
            ret_send.at[rows, :, ret_lanes(g)],
            ret.at[rows, :, ret_lanes(g)],
            send_sem.at[1],
            orecv_sem.at[g],
            {"seq": me},
        )

    for table in tables[:2]:
        table.wait()
    owners = [owner[r] for r in range(requests)]
    places = []
    for r in range(requests):
        rank = jnp.int32(0)
        for e in range(r):
            rank = rank + jnp.where(owners[e] == owners[r], 1, 0)
        places.append(owners[r] * cap + rank)
    parents = [parent_id[r] for r in range(requests)]

    @pl.when(on_decode)
    def _():
        col = iota((1, tokens), 1)
        target = 2 * spread(col >> 1, places) + (col & 1)
        pick = jnp.where(iota((slot_rows, tokens), 0) == target, 1.0, 0.0).astype(jnp.bfloat16)
        tok = iota((tokens, LANES), 0) >> 1
        pid = spread(tok, parents).astype(jnp.float32).astype(jnp.bfloat16)
        pid_slots = jnp.dot(pick, pid, preferred_element_type=jnp.float32)
        for d in range(n_seq):
            slots[d, :, :LANES] = pid_slots[d * per_peer : (d + 1) * per_peer].astype(
                jnp.bfloat16
            )
        block_lanes = 4 * LANES
        for g in range(KV_HEADS):
            load_q[g].wait()
            for c in range(group_width // block_lanes):
                first = g * group_width + c * block_lanes
                part = jnp.dot(
                    pick,
                    q_ref[:, :, first : first + block_lanes].reshape(tokens, block_lanes),
                    preferred_element_type=jnp.float32,
                )
                for d in range(n_seq):
                    slots[d, :, LANES + first : LANES + first + block_lanes] = part[
                        d * per_peer : (d + 1) * per_peer
                    ].astype(jnp.bfloat16)
            if g == 0:
                pl.semaphore_wait(barrier, n_seq)
            for step in range(n_seq - 1, 0, -1):
                slots_to(step, g).start()
        q_to_partner.start()
        arrived[pl.ds(me, 1)] = slots[pl.ds(me, 1)]

    @pl.when(on_prefill)
    def _():
        pl.semaphore_wait(barrier, 1)
        for part in load_q:
            part.wait()

    for table in tables[2:]:
        table.wait()
    lengths = [suffix_len[r] for r in range(requests)]
    lane_page = iota((1, key_count), 1) // PAGE
    group_row = jnp.zeros((1, key_count), jnp.int32)
    base_row = jnp.zeros((1, key_count), jnp.int32)
    suf_pages = suffix_pages.shape[0]
    par_pages = parent_pages.shape[1]
    for j in range(key_count // PAGE):
        page = jnp.where(
            on_prefill,
            suffix_pages[j % suf_pages, j // suf_pages],
            parent_pages[j // par_pages, j % par_pages],
        )
        here = lane_page == page
        group_row = jnp.where(here, jnp.where(on_prefill, j // suf_pages, j // par_pages), group_row)
        base_row = jnp.where(
            here, jnp.where(on_prefill, j % suf_pages, j % par_pages) * PAGE, base_row
        )
    pos_row = base_row + (iota((1, key_count), 1) & (PAGE - 1))
    key_meta[0:1, :] = group_row
    key_meta[1:2, :] = pos_row

    load_step.wait()

    @pl.when(on_prefill)
    def _():
        for c in range(step_ref.shape[1] // (4 * LANES)):
            lanes = slice(c * 4 * LANES, (c + 1) * 4 * LANES)
            step_ref[:, lanes] = step_in[:, :, lanes].reshape(tokens, 4 * LANES)

    cuts = [parent_len[a] for a in range(parent_len.shape[0])]
    load_kv.wait()

    def bias_of(group, limit):
        keep = (key_meta[0:1, :] == group) & (key_meta[1:2, :] < limit)
        return jnp.where(keep, 0.0, MASKED_SCORE)

    def attend(g, query, bias, step_bias=None):
        rows = bias.shape[0]
        ks = slice(g * HEAD_DIM, (g + 1) * HEAD_DIM)
        vs = slice(key_width + g * HEAD_DIM, key_width + (g + 1) * HEAD_DIM)
        contract = (((1,), (1,)), ((), ()))

        def scores(keys, add):
            found = lax.dot_general(query, keys, contract, preferred_element_type=jnp.float32)
            return found.reshape(GROUP, rows, keys.shape[0]) * scale + add[None]

        def blend(term, values):
            term = term.reshape(GROUP * rows, values.shape[0]).astype(jnp.bfloat16)
            mixed = jnp.dot(term, values, preferred_element_type=jnp.float32)
            return mixed.reshape(GROUP, rows, HEAD_DIM)

        score = scores(kv_ref[:, ks], bias)
        top = jnp.max(score, axis=2, keepdims=True)
        if step_bias is not None:
            step_score = scores(step_ref[:, ks], step_bias)
            top = jnp.maximum(top, jnp.max(step_score, axis=2, keepdims=True))
        term = jnp.exp(score - top)
        total = jnp.sum(term, axis=2, keepdims=True)
        mixed = blend(term, kv_ref[:, vs])
        if step_bias is not None:
            step_term = jnp.exp(step_score - top)
            total = total + jnp.sum(step_term, axis=2, keepdims=True)
            mixed = mixed + blend(step_term, step_ref[:, vs])
        return mixed / total, top, total

    def record(g, top, total):
        lane = iota((top.shape[1], LANES), 1)
        stat = jnp.zeros(lane.shape, jnp.float32)
        for h in range(GROUP):
            stat = jnp.where(lane == g * GROUP + h, top[h], stat)
            stat = jnp.where(lane == half + g * GROUP + h, total[h], stat)
        return stat

    def log_sum(stat):
        lane = iota(stat.shape, 1)
        total = jnp.where(lane < heads_all, pltpu.roll(stat, half, 1), 1.0)
        return jnp.where(lane < heads_all, stat, 0.0) + jnp.log(total)

    @pl.when(on_prefill)
    def _():
        row = iota((tokens, 1), 0)
        request = row >> 1
        turn = row & 1
        length = spread(request, lengths)

        def lanes_of(head):
            return slice(head * HEAD_DIM, (head + 1) * HEAD_DIM)

        def own(head):
            return q_ref[:, :, lanes_of(head)].reshape(tokens, HEAD_DIM)

        def passed(head):
            return partner_q[:, :, lanes_of(head)].reshape(tokens, HEAD_DIM)

        def serve(head, value):
            out_ref[:, lanes_of(head)] = value.astype(jnp.bfloat16)

        def keep(head, value):
            near_send[:, lanes_of(head)] = value

        q_to_partner.wait_recv()
        bias = bias_of(request, length)
        step_key = iota((tokens, tokens), 1)
        step_keep = ((step_key >> 1) == request) & ((step_key & 1) < turn + 1)
        step_bias = jnp.where(step_keep, 0.0, MASKED_SCORE)
        stat = jnp.zeros((tokens, LANES), jnp.float32)
        for g in range(KV_HEADS):
            heads = range(g * GROUP, (g + 1) * GROUP)
            query = jnp.concatenate([passed(head) for head in heads], axis=0)
            mixed, top, total = attend(g, query, bias, step_bias)
            for h, head in enumerate(heads):
                keep(head, mixed[h])
            stat = stat + record(g, top, total)
        near_stat_send[...] = log_sum(stat)
        o_to_partner.start()
        s_to_partner.start()
        bias = bias_of(request, length - 1 + turn)
        for g in range(KV_HEADS):
            heads = range(g * GROUP, (g + 1) * GROUP)
            query = jnp.concatenate([own(head) for head in heads], axis=0)
            mixed, _, _ = attend(g, query, bias)
            for h, head in enumerate(heads):
                serve(head, mixed[h])
        s_to_partner.wait_send()
        o_to_partner.wait_send()

    batch = min(8, n_seq)

    def answer(c, g, batch):
        batch_rows = batch * per_peer
        steps = [n_seq - 1 - batch * c - i for i in range(batch)]
        peers = [peer_at(step) for step in steps]
        rows = pl.ds(c * batch_rows, batch_rows)
        for step in steps[::unit]:
            if not isinstance(step, int):
                pl.when(step // unit > 0)(lambda: slots_from(step // unit, g, unit).wait_recv())
                pl.when(step // unit == 0)(lambda: slots_from(0, g, unit - 1).wait_recv())
            else:
                slots_from(step // unit, g, unit if step >= unit else unit - 1).wait_recv()

        def gathered(first):
            return jnp.concatenate(
                [
                    arrived[peer, :, first : first + LANES].astype(jnp.float32) for peer in peers
                ],
                axis=0,
            )

        if g == 0:
            group = gathered(0).astype(jnp.int32)[:, 0:1]
            slot_bias[rows, :] = bias_of(group, spread(group, cuts))
        query = jnp.concatenate(
            [
                gathered(LANES + head * HEAD_DIM).astype(jnp.bfloat16)
                for head in range(g * GROUP, (g + 1) * GROUP)
            ],
            axis=0,
        )
        mixed, top, total = attend(g, query, slot_bias[rows, :])
        for h in range(GROUP):
            head = g * GROUP + h
            for i, peer in enumerate(peers):
                ret_send[peer, :, head * HEAD_DIM : (head + 1) * HEAD_DIM] = mixed[
                    h, i * per_peer : (i + 1) * per_peer
                ].astype(jnp.bfloat16)
        stat = record(g, top, total)
        if g > 0:
            stat = stat + slot_stat[rows, :]
        if g < KV_HEADS - 1:
            slot_stat[rows, :] = stat
        else:
            value = log_sum(stat)
            high = value.astype(jnp.bfloat16).astype(jnp.float32)
            rest = value - high
            middle = rest.astype(jnp.bfloat16).astype(jnp.float32)
            low = rest - middle
            lane = iota(value.shape, 1)
            packed = jnp.where(
                lane < heads_all,
                high,
                jnp.where(
                    lane < 2 * heads_all,
                    pltpu.roll(middle, heads_all, 1),
                    pltpu.roll(low, 2 * heads_all, 1),
                ),
            )
            for i, peer in enumerate(peers):
                ret_send[peer, :, q_width:] = packed[
                    i * per_peer : (i + 1) * per_peer
                ].astype(jnp.bfloat16)

        for step, peer in zip(steps, peers):
            if isinstance(step, int):
                if step > 0:
                    out_to(peer, g).start()
            else:
                pl.when(step > 0)(lambda peer=peer: out_to(peer, g).start())

    @pl.when(on_decode)
    def _():
        for g in range(KV_HEADS):
            if n_seq == batch:
                pieces = (1, 1, 1, 2)[g] if batch % 2 == 0 else 1
                for c in range(pieces):
                    answer(c, g, batch // pieces)
            else:
                each(0, n_seq // batch, lambda c: answer(c, g, batch))

    @pl.when(on_decode)
    def _():
        ret[pl.ds(me, 1)] = ret_send[pl.ds(me, 1)]
        tok = iota((tokens, 1), 0)
        target = 2 * spread(tok >> 1, places) + (tok & 1)
        unpick = jnp.where(iota((tokens, slot_rows), 1) == target, 1.0, 0.0)
        o_to_partner.wait_recv()
        s_to_partner.wait_recv()
        pick_back = unpick.astype(jnp.bfloat16)

        def came(first):
            rows = jnp.concatenate(
                [ret[s, :, first : first + LANES].astype(jnp.float32) for s in range(n_seq)],
                axis=0,
            ).astype(jnp.bfloat16)
            return jnp.dot(pick_back, rows, preferred_element_type=jnp.float32)

        for g in range(KV_HEADS):
            out_from(g).wait_recv()
            for head in range(g * GROUP, (g + 1) * GROUP):
                far_out[:, head * HEAD_DIM : (head + 1) * HEAD_DIM] = came(head * HEAD_DIM)
        parts = came(q_width)
        far = (
            parts
            + pltpu.roll(parts, LANES - heads_all, 1)
            + pltpu.roll(parts, LANES - 2 * heads_all, 1)
        )
        near = partner_stat[...]
        top = jnp.maximum(far, near)
        far_weight = jnp.exp(far - top)
        far_share = far_weight / (far_weight + jnp.exp(near - top))
        for head in range(heads_all):
            part = slice(head * HEAD_DIM, (head + 1) * HEAD_DIM)
            close = partner_o[:, part]
            out_ref[:, part] = (
                close + (far_out[:, part] - close) * far_share[:, head : head + 1]
            ).astype(jnp.bfloat16)
        q_to_partner.wait_send()
        rows = pl.ds(0, n_seq - 1)
        remote(
            slots.at[rows], arrived.at[rows], send_sem.at[0], recv_sem.at[0, 0], {"seq": me}
        ).wait_send()
        remote(
            ret_send.at[rows], ret.at[rows], send_sem.at[1], orecv_sem.at[0], {"seq": me}
        ).wait_send()


def local(
    kv_store, queries, step_kv, suffix_pages, suffix_len, owner, parent_id, parent_pages, parent_len
):
    n_seq = lax.axis_size("seq")
    page_store = kv_store[0]
    requests, turns, q_width = queries.shape[1:]
    tokens = requests * turns
    cap = max(4, 2 * requests // n_seq)
    per_peer = 2 * cap
    units = n_seq // min(4, n_seq)
    bf16, f32 = jnp.bfloat16, jnp.float32
    vmem = pl.BlockSpec(memory_space=pltpu.VMEM)
    hbm = pl.BlockSpec(memory_space=pl.ANY)
    dma = pltpu.SemaphoreType.DMA
    served = pl.pallas_call(
        functools.partial(kernel, n_seq, cap),
        out_shape=pltpu.VMEM((tokens, q_width), bf16),
        in_specs=[hbm] * 9,
        out_specs=vmem,
        scratch_shapes=[
            pltpu.SMEM((requests,), jnp.int32),
            pltpu.SMEM((requests,), jnp.int32),
            pltpu.SMEM((requests,), jnp.int32),
            pltpu.SMEM(suffix_pages.shape[::-1], jnp.int32),
            pltpu.SMEM(parent_pages.shape, jnp.int32),
            pltpu.SMEM(parent_len.shape, jnp.int32),
            pltpu.VMEM((requests, turns, q_width), bf16),
            pltpu.VMEM(page_store.shape, bf16),
            pltpu.VMEM(step_kv.shape, bf16),
            pltpu.VMEM((tokens, step_kv.shape[2]), bf16),
            pltpu.VMEM((n_seq, per_peer, q_width + LANES), bf16),
            pltpu.VMEM((n_seq, per_peer, q_width + LANES), bf16),
            pltpu.VMEM((8, page_store.shape[0]), jnp.int32),
            pltpu.VMEM((n_seq * per_peer, page_store.shape[0]), f32),
            pltpu.VMEM((n_seq * per_peer, LANES), f32),
            pltpu.VMEM((tokens, q_width), f32),
            pltpu.VMEM((tokens, q_width), f32),
            pltpu.VMEM((tokens, LANES), f32),
            pltpu.VMEM((n_seq, per_peer, q_width + LANES), bf16),
            pltpu.VMEM((n_seq, per_peer, q_width + LANES), bf16),
            pltpu.VMEM((requests, turns, q_width), bf16),
            pltpu.VMEM((tokens, q_width), f32),
            pltpu.VMEM((tokens, LANES), f32),
            dma((8 + KV_HEADS,)),
            dma((2,)),
            dma((units, KV_HEADS)),
            dma((KV_HEADS,)),
            dma((3,)),
            dma((3,)),
        ],
        compiler_params=pltpu.CompilerParams(
            collective_id=0, has_side_effects=True, vmem_limit_bytes=60 * 1024 * 1024
        ),
    )(
        owner.reshape(-1),
        parent_id,
        suffix_len,
        suffix_pages.T,
        parent_pages,
        parent_len,
        queries[0],
        page_store,
        step_kv,
    )
    return served.reshape(1, requests, turns, q_width)


def solution(mesh):
    in_specs = (
        P("role", ("groups", "seq"), None),
        P("role", ("groups", "seq"), None, None),
        P(("groups", "seq"), None, None),
        P(("groups", "seq"), None),
        P(("groups", "seq")),
        P(("groups", "seq"), None),
        P(("groups", "seq")),
        P(("groups", "seq"), None),
        P(("groups", "seq")),
    )
    out_specs = P("role", ("groups", "seq"), None, None)
    return jax.shard_map(local, mesh=mesh, in_specs=in_specs, out_specs=out_specs, check_vma=False)
```

```python
import functools

import jax
import jax.numpy as jnp
from jax import lax
from jax.experimental import pallas as pl
from jax.experimental.pallas import tpu as pltpu
from jax.sharding import PartitionSpec as P

HEAD_DIM = 128
KV_HEADS = 4
GROUP = 8
PAGE = 16
LANES = 128

MASKED_SCORE = -1e30
MESH = pl.DeviceIdType.MESH


def iota(shape, dim):
    return lax.broadcasted_iota(jnp.int32, shape, dim)


def spread(index, scalars):
    out = jnp.zeros(index.shape, jnp.int32)
    for i, scalar in enumerate(scalars):
        out = jnp.where(index == i, scalar, out)
    return out


def kernel(
    n_seq,
    cap,
    owner_hbm,
    parent_id_hbm,
    suffix_len_hbm,
    suffix_pages_hbm,
    parent_pages_hbm,
    parent_len_hbm,
    q_hbm,
    kv_hbm,
    step_hbm,
    out_ref,
    owner,
    parent_id,
    suffix_len,
    suffix_pages,
    parent_pages,
    parent_len,
    q_ref,
    kv_ref,
    step_in,
    step_ref,
    slots,
    arrived,
    key_meta,
    slot_bias,
    slot_stat,
    far_out,
    near_send,
    near_stat_send,
    ret_send,
    ret,
    partner_q,
    partner_o,
    partner_stat,
    load_sem,
    send_sem,
    recv_sem,
    orecv_sem,
    psend_sem,
    precv_sem,
):
    role = lax.axis_index("role")
    me = lax.axis_index("seq")
    requests, turns, q_width = q_ref.shape
    tokens = requests * turns
    per_peer = 2 * cap
    slot_rows = n_seq * per_peer
    key_count = kv_ref.shape[0]
    key_width = KV_HEADS * HEAD_DIM
    scale = HEAD_DIM ** (-0.5)
    partner = {"role": 1 - role}
    on_decode = role == 1
    on_prefill = role == 0
    heads_all = KV_HEADS * GROUP
    group_width = GROUP * HEAD_DIM
    half = LANES // 2
    quad = min(4, n_seq)
    my_quad = me // quad * quad
    bits = [(me // 2**b) % 2 for b in range(n_seq.bit_length() - 1)]

    def peer_at(step):
        peer = me
        for b, mine in enumerate(bits):
            if isinstance(step, int):
                if (step >> b) & 1:
                    peer = peer + 2**b * (1 - 2 * mine)
            else:
                peer = peer + 2**b * (1 - 2 * mine) * ((step // 2**b) % 2)
        return peer

    def each(first, last, action):
        def body(i, carry):
            action(i)
            return carry

        lax.fori_loop(first, last, body, 0)

    barrier = pltpu.get_barrier_semaphore()

    def greet(peer):
        pl.semaphore_signal(barrier, inc=1, device_id={"seq": peer}, device_id_type=MESH)

    pl.semaphore_signal(barrier, inc=1, device_id=partner, device_id_type=MESH)

    @pl.when(on_decode)
    def _():
        for step in range(n_seq - 1, 0, -1):
            greet(peer_at(step))

    tables = [
        pltpu.make_async_copy(src, dst, load_sem.at[i])
        for i, (src, dst) in enumerate(
            (
                (owner_hbm, owner),
                (parent_id_hbm, parent_id),
                (suffix_len_hbm, suffix_len),
                (suffix_pages_hbm, suffix_pages),
                (parent_pages_hbm, parent_pages),
                (parent_len_hbm, parent_len),
            )
        )
    ]
    load_step = pltpu.make_async_copy(step_hbm, step_in, load_sem.at[6])
    load_kv = pltpu.make_async_copy(kv_hbm, kv_ref, load_sem.at[7])

    def out_lanes(g):
        return slice(g * group_width, (g + 1) * group_width)

    load_q = [
        pltpu.make_async_copy(
            q_hbm.at[:, :, out_lanes(g)], q_ref.at[:, :, out_lanes(g)], load_sem.at[8 + g]
        )
        for g in range(KV_HEADS)
    ]
    for table in tables[:2]:
        table.start()
    for part in load_q:
        part.start()
    for table in tables[2:]:
        table.start()
    load_kv.start()
    load_step.start()

    def remote(src, dst, ssem, rsem, device):
        return pltpu.make_async_remote_copy(
            src_ref=src,
            dst_ref=dst,
            send_sem=ssem,
            recv_sem=rsem,
            device_id=device,
            device_id_type=MESH,
        )

    q_to_partner = remote(q_ref, partner_q, psend_sem.at[0], precv_sem.at[0], partner)
    o_to_partner = remote(near_send, partner_o, psend_sem.at[1], precv_sem.at[1], partner)
    s_to_partner = remote(near_stat_send, partner_stat, psend_sem.at[2], precv_sem.at[2], partner)

    def q_lanes(g):
        first = 0 if g == 0 else LANES + g * group_width
        return slice(first, LANES + (g + 1) * group_width)

    def ret_lanes(g):
        last = LANES if g == KV_HEADS - 1 else 0
        return slice(g * group_width, (g + 1) * group_width + last)

    def slots_to(step, g):
        peer = peer_at(step)
        return remote(
            slots.at[peer, :, q_lanes(g)],
            arrived.at[me, :, q_lanes(g)],
            send_sem.at[0],
            recv_sem.at[me // 2, g],
            {"seq": peer},
        )

    def slots_from(u, g, count):
        rows = pl.ds(0, count)
        return remote(
            slots.at[rows, :, q_lanes(g)],
            arrived.at[rows, :, q_lanes(g)],
            send_sem.at[0],
            recv_sem.at[u, g],
            {"seq": me},
        )

    def out_to(peer, g):
        return remote(
            ret_send.at[peer, :, ret_lanes(g)],
            ret.at[me, :, ret_lanes(g)],
            send_sem.at[1],
            orecv_sem.at[g],
            {"seq": peer},
        )

    def out_from(g):
        rows = pl.ds(0, n_seq - 1)
        return remote(
            ret_send.at[rows, :, ret_lanes(g)],
            ret.at[rows, :, ret_lanes(g)],
            send_sem.at[1],
            orecv_sem.at[g],
            {"seq": me},
        )

    for table in tables[:2]:
        table.wait()
    owners = [owner[r] for r in range(requests)]
    places = []
    for r in range(requests):
        rank = jnp.int32(0)
        for e in range(r):
            rank = rank + jnp.where(owners[e] == owners[r], 1, 0)
        places.append(owners[r] * cap + rank)
    parents = [parent_id[r] for r in range(requests)]

    @pl.when(on_decode)
    def _():
        col = iota((1, tokens), 1)
        target = 2 * spread(col >> 1, places) + (col & 1)
        pick = jnp.where(iota((slot_rows, tokens), 0) == target, 1.0, 0.0).astype(jnp.bfloat16)
        tok = iota((tokens, LANES), 0) >> 1
        pid = spread(tok, parents).astype(jnp.float32).astype(jnp.bfloat16)
        pid_slots = jnp.dot(pick, pid, preferred_element_type=jnp.float32)
        for d in range(n_seq):
            slots[d, :, :LANES] = pid_slots[d * per_peer : (d + 1) * per_peer].astype(
                jnp.bfloat16
            )
        block_lanes = 4 * LANES
        for g in range(KV_HEADS):
            load_q[g].wait()
            for c in range(group_width // block_lanes):
                first = g * group_width + c * block_lanes
                part = jnp.dot(
                    pick,
                    q_ref[:, :, first : first + block_lanes].reshape(tokens, block_lanes),
                    preferred_element_type=jnp.float32,
                )
                for d in range(n_seq):
                    slots[d, :, LANES + first : LANES + first + block_lanes] = part[
                        d * per_peer : (d + 1) * per_peer
                    ].astype(jnp.bfloat16)
            if g == 0:
                pl.semaphore_wait(barrier, n_seq)
            for step in range(n_seq - 1, 0, -1):
                slots_to(step, g).start()
        q_to_partner.start()
        arrived[pl.ds(me, 1)] = slots[pl.ds(me, 1)]

    @pl.when(on_prefill)
    def _():
        pl.semaphore_wait(barrier, 1)
        for part in load_q:
            part.wait()

    for table in tables[2:]:
        table.wait()
    lengths = [suffix_len[r] for r in range(requests)]
    lane_page = iota((1, key_count), 1) // PAGE
    group_row = jnp.zeros((1, key_count), jnp.int32)
    base_row = jnp.zeros((1, key_count), jnp.int32)
    suf_pages = suffix_pages.shape[0]
    par_pages = parent_pages.shape[1]
    for j in range(key_count // PAGE):
        page = jnp.where(
            on_prefill,
            suffix_pages[j % suf_pages, j // suf_pages],
            parent_pages[j // par_pages, j % par_pages],
        )
        here = lane_page == page
        group_row = jnp.where(here, jnp.where(on_prefill, j // suf_pages, j // par_pages), group_row)
        base_row = jnp.where(
            here, jnp.where(on_prefill, j % suf_pages, j % par_pages) * PAGE, base_row
        )
    pos_row = base_row + (iota((1, key_count), 1) & (PAGE - 1))
    key_meta[0:1, :] = group_row
    key_meta[1:2, :] = pos_row

    load_step.wait()

    @pl.when(on_prefill)
    def _():
        for c in range(step_ref.shape[1] // (4 * LANES)):
            lanes = slice(c * 4 * LANES, (c + 1) * 4 * LANES)
            step_ref[:, lanes] = step_in[:, :, lanes].reshape(tokens, 4 * LANES)

    cuts = [parent_len[a] for a in range(parent_len.shape[0])]
    load_kv.wait()

    def bias_of(group, limit):
        keep = (key_meta[0:1, :] == group) & (key_meta[1:2, :] < limit)
        return jnp.where(keep, 0.0, MASKED_SCORE)

    def attend(g, query, bias, step_bias=None):
        rows = bias.shape[0]
        ks = slice(g * HEAD_DIM, (g + 1) * HEAD_DIM)
        vs = slice(key_width + g * HEAD_DIM, key_width + (g + 1) * HEAD_DIM)
        contract = (((1,), (1,)), ((), ()))

        def scores(keys, add):
            found = lax.dot_general(query, keys, contract, preferred_element_type=jnp.float32)
            return found.reshape(GROUP, rows, keys.shape[0]) * scale + add[None]

        def blend(term, values):
            term = term.reshape(GROUP * rows, values.shape[0]).astype(jnp.bfloat16)
            mixed = jnp.dot(term, values, preferred_element_type=jnp.float32)
            return mixed.reshape(GROUP, rows, HEAD_DIM)

        score = scores(kv_ref[:, ks], bias)
        top = jnp.max(score, axis=2, keepdims=True)
        if step_bias is not None:
            step_score = scores(step_ref[:, ks], step_bias)
            top = jnp.maximum(top, jnp.max(step_score, axis=2, keepdims=True))
        term = jnp.exp(score - top)
        total = jnp.sum(term, axis=2, keepdims=True)
        mixed = blend(term, kv_ref[:, vs])
        if step_bias is not None:
            step_term = jnp.exp(step_score - top)
            total = total + jnp.sum(step_term, axis=2, keepdims=True)
            mixed = mixed + blend(step_term, step_ref[:, vs])
        return mixed / total, top, total

    def record(g, top, total):
        lane = iota((top.shape[1], LANES), 1)
        stat = jnp.zeros(lane.shape, jnp.float32)
        for h in range(GROUP):
            stat = jnp.where(lane == g * GROUP + h, top[h], stat)
            stat = jnp.where(lane == half + g * GROUP + h, total[h], stat)
        return stat

    def log_sum(stat):
        lane = iota(stat.shape, 1)
        total = jnp.where(lane < heads_all, pltpu.roll(stat, half, 1), 1.0)
        return jnp.where(lane < heads_all, stat, 0.0) + jnp.log(total)

    @pl.when(on_prefill)
    def _():
        row = iota((tokens, 1), 0)
        request = row >> 1
        turn = row & 1
        length = spread(request, lengths)

        def lanes_of(head):
            return slice(head * HEAD_DIM, (head + 1) * HEAD_DIM)

        def own(head):
            return q_ref[:, :, lanes_of(head)].reshape(tokens, HEAD_DIM)

        def passed(head):
            return partner_q[:, :, lanes_of(head)].reshape(tokens, HEAD_DIM)

        def serve(head, value):
            out_ref[:, lanes_of(head)] = value.astype(jnp.bfloat16)

        def keep(head, value):
            near_send[:, lanes_of(head)] = value

        q_to_partner.wait_recv()
        bias = bias_of(request, length)
        step_key = iota((tokens, tokens), 1)
        step_keep = ((step_key >> 1) == request) & ((step_key & 1) < turn + 1)
        step_bias = jnp.where(step_keep, 0.0, MASKED_SCORE)
        stat = jnp.zeros((tokens, LANES), jnp.float32)
        for g in range(KV_HEADS):
            heads = range(g * GROUP, (g + 1) * GROUP)
            query = jnp.concatenate([passed(head) for head in heads], axis=0)
            mixed, top, total = attend(g, query, bias, step_bias)
            for h, head in enumerate(heads):
                keep(head, mixed[h])
            stat = stat + record(g, top, total)
        near_stat_send[...] = log_sum(stat)
        o_to_partner.start()
        s_to_partner.start()
        bias = bias_of(request, length - 1 + turn)
        for g in range(KV_HEADS):
            heads = range(g * GROUP, (g + 1) * GROUP)
            query = jnp.concatenate([own(head) for head in heads], axis=0)
            mixed, _, _ = attend(g, query, bias)
            for h, head in enumerate(heads):
                serve(head, mixed[h])
        s_to_partner.wait_send()
        o_to_partner.wait_send()

    def answer(first, count, g, mine):
        peers = [first + i for i in range(count)]
        rows = pl.ds(first * per_peer, count * per_peer)
        for pair in [first // 2 + i for i in range(count // 2)]:
            if mine:
                pl.when(pair == me // 2)(lambda: slots_from(pair, g, 1).wait_recv())
                pl.when(pair != me // 2)(lambda: slots_from(pair, g, 2).wait_recv())
            else:
                slots_from(pair, g, 2).wait_recv()

        def gathered(first):
            return jnp.concatenate(
                [
                    arrived[peer, :, first : first + LANES].astype(jnp.float32) for peer in peers
                ],
                axis=0,
            )

        if g == 0:
            group = gathered(0).astype(jnp.int32)[:, 0:1]
            slot_bias[rows, :] = bias_of(group, spread(group, cuts))
        query = jnp.concatenate(
            [
                gathered(LANES + head * HEAD_DIM).astype(jnp.bfloat16)
                for head in range(g * GROUP, (g + 1) * GROUP)
            ],
            axis=0,
        )
        mixed, top, total = attend(g, query, slot_bias[rows, :])
        for h in range(GROUP):
            head = g * GROUP + h
            for i, peer in enumerate(peers):
                ret_send[peer, :, head * HEAD_DIM : (head + 1) * HEAD_DIM] = mixed[
                    h, i * per_peer : (i + 1) * per_peer
                ].astype(jnp.bfloat16)
        stat = record(g, top, total)
        if g > 0:
            stat = stat + slot_stat[rows, :]
        if g < KV_HEADS - 1:
            slot_stat[rows, :] = stat
        else:
            value = log_sum(stat)
            high = value.astype(jnp.bfloat16).astype(jnp.float32)
            rest = value - high
            middle = rest.astype(jnp.bfloat16).astype(jnp.float32)
            low = rest - middle
            lane = iota(value.shape, 1)
            packed = jnp.where(
                lane < heads_all,
                high,
                jnp.where(
                    lane < 2 * heads_all,
                    pltpu.roll(middle, heads_all, 1),
                    pltpu.roll(low, 2 * heads_all, 1),
                ),
            )
            for i, peer in enumerate(peers):
                ret_send[peer, :, q_width:] = packed[
                    i * per_peer : (i + 1) * per_peer
                ].astype(jnp.bfloat16)

        for peer in peers:
            if mine:
                pl.when(peer != me)(lambda: out_to(peer, g).start())
            else:
                out_to(peer, g).start()

    @pl.when(on_decode)
    def _():
        if n_seq == 2 * quad == 8:
            upper = me // quad
            starts = [my_quad, 4 - 2 * upper, 6 - 6 * upper, 4 - 4 * upper]
            for kind, g in [(3, 0), (0, 0), (3, 1), (0, 1), (3, 2), (0, 2), (2, 3), (1, 3), (0, 3)]:
                answer(starts[kind], (4, 2, 2, 4)[kind], g, kind == 0)
        else:
            for g in range(KV_HEADS):
                answer(my_quad, quad, g, True)
                each(
                    1,
                    n_seq // quad,
                    lambda i: answer(lax.rem(my_quad + i * quad, n_seq), quad, g, False),
                )

    @pl.when(on_decode)
    def _():
        ret[pl.ds(me, 1)] = ret_send[pl.ds(me, 1)]
        tok = iota((tokens, 1), 0)
        target = 2 * spread(tok >> 1, places) + (tok & 1)
        unpick = jnp.where(iota((tokens, slot_rows), 1) == target, 1.0, 0.0)
        o_to_partner.wait_recv()
        s_to_partner.wait_recv()
        pick_back = unpick.astype(jnp.bfloat16)

        def came(first):
            rows = jnp.concatenate(
                [ret[s, :, first : first + LANES].astype(jnp.float32) for s in range(n_seq)],
                axis=0,
            ).astype(jnp.bfloat16)
            return jnp.dot(pick_back, rows, preferred_element_type=jnp.float32)

        last = KV_HEADS - 1
        for g in range(last):
            out_from(g).wait_recv()
            for head in range(g * GROUP, (g + 1) * GROUP):
                far_out[:, head * HEAD_DIM : (head + 1) * HEAD_DIM] = came(head * HEAD_DIM)
        out_from(last).wait_recv()
        parts = came(q_width)
        far = (
            parts
            + pltpu.roll(parts, LANES - heads_all, 1)
            + pltpu.roll(parts, LANES - 2 * heads_all, 1)
        )
        near = partner_stat[...]
        top = jnp.maximum(far, near)
        far_weight = jnp.exp(far - top)
        far_share = far_weight / (far_weight + jnp.exp(near - top))
        for head in range(heads_all):
            part = slice(head * HEAD_DIM, (head + 1) * HEAD_DIM)
            close = partner_o[:, part]
            distant = came(head * HEAD_DIM) if head // GROUP == last else far_out[:, part]
            out_ref[:, part] = (
                close + (distant - close) * far_share[:, head : head + 1]
            ).astype(jnp.bfloat16)
        q_to_partner.wait_send()
        rows = pl.ds(0, n_seq - 1)
        remote(
            slots.at[rows], arrived.at[rows], send_sem.at[0], recv_sem.at[0, 0], {"seq": me}
        ).wait_send()
        remote(
            ret_send.at[rows], ret.at[rows], send_sem.at[1], orecv_sem.at[0], {"seq": me}
        ).wait_send()


def local(
    kv_store, queries, step_kv, suffix_pages, suffix_len, owner, parent_id, parent_pages, parent_len
):
    n_seq = lax.axis_size("seq")
    page_store = kv_store[0]
    requests, turns, q_width = queries.shape[1:]
    tokens = requests * turns
    cap = max(4, 2 * requests // n_seq)
    per_peer = 2 * cap
    bf16, f32 = jnp.bfloat16, jnp.float32
    vmem = pl.BlockSpec(memory_space=pltpu.VMEM)
    hbm = pl.BlockSpec(memory_space=pl.ANY)
    dma = pltpu.SemaphoreType.DMA
    served = pl.pallas_call(
        functools.partial(kernel, n_seq, cap),
        out_shape=pltpu.VMEM((tokens, q_width), bf16),
        in_specs=[hbm] * 9,
        out_specs=vmem,
        scratch_shapes=[
            pltpu.SMEM((requests,), jnp.int32),
            pltpu.SMEM((requests,), jnp.int32),
            pltpu.SMEM((requests,), jnp.int32),
            pltpu.SMEM(suffix_pages.shape[::-1], jnp.int32),
            pltpu.SMEM(parent_pages.shape, jnp.int32),
            pltpu.SMEM(parent_len.shape, jnp.int32),
            pltpu.VMEM((requests, turns, q_width), bf16),
            pltpu.VMEM(page_store.shape, bf16),
            pltpu.VMEM(step_kv.shape, bf16),
            pltpu.VMEM((tokens, step_kv.shape[2]), bf16),
            pltpu.VMEM((n_seq, per_peer, q_width + LANES), bf16),
            pltpu.VMEM((n_seq, per_peer, q_width + LANES), bf16),
            pltpu.VMEM((8, page_store.shape[0]), jnp.int32),
            pltpu.VMEM((n_seq * per_peer, page_store.shape[0]), f32),
            pltpu.VMEM((n_seq * per_peer, LANES), f32),
            pltpu.VMEM((tokens, q_width), f32),
            pltpu.VMEM((tokens, q_width), f32),
            pltpu.VMEM((tokens, LANES), f32),
            pltpu.VMEM((n_seq, per_peer, q_width + LANES), bf16),
            pltpu.VMEM((n_seq, per_peer, q_width + LANES), bf16),
            pltpu.VMEM((requests, turns, q_width), bf16),
            pltpu.VMEM((tokens, q_width), f32),
            pltpu.VMEM((tokens, LANES), f32),
            dma((8 + KV_HEADS,)),
            dma((2,)),
            dma((n_seq // 2, KV_HEADS)),
            dma((KV_HEADS,)),
            dma((3,)),
            dma((3,)),
        ],
        compiler_params=pltpu.CompilerParams(
            collective_id=0, has_side_effects=True, vmem_limit_bytes=60 * 1024 * 1024
        ),
    )(
        owner.reshape(-1),
        parent_id,
        suffix_len,
        suffix_pages.T,
        parent_pages,
        parent_len,
        queries[0],
        page_store,
        step_kv,
    )
    return served.reshape(1, requests, turns, q_width)


def solution(mesh):
    in_specs = (
        P("role", ("groups", "seq"), None),
        P("role", ("groups", "seq"), None, None),
        P(("groups", "seq"), None, None),
        P(("groups", "seq"), None),
        P(("groups", "seq")),
        P(("groups", "seq"), None),
        P(("groups", "seq")),
        P(("groups", "seq"), None),
        P(("groups", "seq")),
    )
    out_specs = P("role", ("groups", "seq"), None, None)
    return jax.shard_map(local, mesh=mesh, in_specs=in_specs, out_specs=out_specs, check_vma=False)
```

```python
import functools

import jax
import jax.numpy as jnp
from jax import lax
from jax.experimental import pallas as pl
from jax.experimental.pallas import tpu as pltpu
from jax.sharding import PartitionSpec as P

HEAD_DIM = 128
KV_HEADS = 4
GROUP = 8
PAGE = 16
LANES = 128

MASKED_SCORE = -1e30
MESH = pl.DeviceIdType.MESH


def iota(shape, dim):
    return lax.broadcasted_iota(jnp.int32, shape, dim)


def spread(index, scalars):
    out = jnp.zeros(index.shape, jnp.int32)
    for i, scalar in enumerate(scalars):
        out = jnp.where(index == i, scalar, out)
    return out


def kernel(
    n_seq,
    cap,
    owner_hbm,
    parent_id_hbm,
    suffix_len_hbm,
    suffix_pages_hbm,
    parent_pages_hbm,
    parent_len_hbm,
    q_hbm,
    kv_hbm,
    step_hbm,
    out_ref,
    owner,
    parent_id,
    suffix_len,
    suffix_pages,
    parent_pages,
    parent_len,
    q_ref,
    kv_ref,
    step_in,
    step_ref,
    slots,
    arrived,
    key_meta,
    slot_bias,
    slot_stat,
    far_out,
    near_send,
    ret_send,
    ret,
    partner_q,
    partner_o,
    load_sem,
    send_sem,
    recv_sem,
    orecv_sem,
    psend_sem,
    precv_sem,
):
    role = lax.axis_index("role")
    me = lax.axis_index("seq")
    requests, turns, q_width = q_ref.shape
    tokens = requests * turns
    per_peer = 2 * cap
    slot_rows = n_seq * per_peer
    key_count = kv_ref.shape[0]
    key_width = KV_HEADS * HEAD_DIM
    scale = HEAD_DIM ** (-0.5)
    partner = {"role": 1 - role}
    on_decode = role == 1
    on_prefill = role == 0
    heads_all = KV_HEADS * GROUP
    group_width = GROUP * HEAD_DIM
    half = LANES // 2
    quad = min(4, n_seq)
    my_quad = me // quad * quad
    bits = [(me // 2**b) % 2 for b in range(n_seq.bit_length() - 1)]

    def peer_at(step):
        peer = me
        for b, mine in enumerate(bits):
            if isinstance(step, int):
                if (step >> b) & 1:
                    peer = peer + 2**b * (1 - 2 * mine)
            else:
                peer = peer + 2**b * (1 - 2 * mine) * ((step // 2**b) % 2)
        return peer

    def each(first, last, action):
        def body(i, carry):
            action(i)
            return carry

        lax.fori_loop(first, last, body, 0)

    barrier = pltpu.get_barrier_semaphore()

    def greet(peer):
        pl.semaphore_signal(barrier, inc=1, device_id={"seq": peer}, device_id_type=MESH)

    pl.semaphore_signal(barrier, inc=1, device_id=partner, device_id_type=MESH)

    @pl.when(on_decode)
    def _():
        for step in range(n_seq - 1, 0, -1):
            greet(peer_at(step))

    tables = [
        pltpu.make_async_copy(src, dst, load_sem.at[i])
        for i, (src, dst) in enumerate(
            (
                (owner_hbm, owner),
                (parent_id_hbm, parent_id),
                (suffix_len_hbm, suffix_len),
                (suffix_pages_hbm, suffix_pages),
                (parent_pages_hbm, parent_pages),
                (parent_len_hbm, parent_len),
            )
        )
    ]
    load_step = pltpu.make_async_copy(step_hbm, step_in, load_sem.at[6])
    load_kv = pltpu.make_async_copy(kv_hbm, kv_ref, load_sem.at[7])

    def out_lanes(g):
        return slice(g * group_width, (g + 1) * group_width)

    load_q = [
        pltpu.make_async_copy(
            q_hbm.at[:, :, lanes], q_ref.at[:, :, lanes], load_sem.at[8 + i]
        )
        for i, lanes in enumerate((slice(0, group_width), slice(group_width, q_width)))
    ]
    for table in tables[:2]:
        table.start()
    for part in load_q:
        part.start()
    for table in tables[2:]:
        table.start()
    load_kv.start()
    load_step.start()

    def remote(src, dst, ssem, rsem, device):
        return pltpu.make_async_remote_copy(
            src_ref=src,
            dst_ref=dst,
            send_sem=ssem,
            recv_sem=rsem,
            device_id=device,
            device_id_type=MESH,
        )

    q_to_partner = remote(q_ref, partner_q, psend_sem.at[0], precv_sem.at[0], partner)
    o_to_partner = remote(near_send, partner_o, psend_sem.at[1], precv_sem.at[1], partner)

    def q_lanes(g):
        first = 0 if g == 0 else LANES + g * group_width
        return slice(first, LANES + (g + 1) * group_width)

    def ret_lanes(g):
        last = LANES if g == KV_HEADS - 1 else 0
        return slice(g * group_width, (g + 1) * group_width + last)

    def slots_to(step, g):
        peer = peer_at(step)
        return remote(
            slots.at[peer, :, q_lanes(g)],
            arrived.at[me, :, q_lanes(g)],
            send_sem.at[0],
            recv_sem.at[me // quad, g],
            {"seq": peer},
        )

    def slots_from(u, g, count):
        rows = pl.ds(0, count)
        return remote(
            slots.at[rows, :, q_lanes(g)],
            arrived.at[rows, :, q_lanes(g)],
            send_sem.at[0],
            recv_sem.at[u, g],
            {"seq": me},
        )

    def out_to(peer, g):
        return remote(
            ret_send.at[peer, :, ret_lanes(g)],
            ret.at[me, :, ret_lanes(g)],
            send_sem.at[1],
            orecv_sem.at[g],
            {"seq": peer},
        )

    def out_from(g):
        rows = pl.ds(0, n_seq - 1)
        return remote(
            ret_send.at[rows, :, ret_lanes(g)],
            ret.at[rows, :, ret_lanes(g)],
            send_sem.at[1],
            orecv_sem.at[g],
            {"seq": me},
        )

    for table in tables[:2]:
        table.wait()
    owners = [owner[r] for r in range(requests)]
    places = []
    for r in range(requests):
        rank = jnp.int32(0)
        for e in range(r):
            rank = rank + jnp.where(owners[e] == owners[r], 1, 0)
        places.append(owners[r] * cap + rank)
    parents = [parent_id[r] for r in range(requests)]

    @pl.when(on_decode)
    def _():
        col = iota((1, tokens), 1)
        target = 2 * spread(col >> 1, places) + (col & 1)
        pick = jnp.where(iota((slot_rows, tokens), 0) == target, 1.0, 0.0).astype(jnp.bfloat16)
        tok = iota((tokens, LANES), 0) >> 1
        pid = spread(tok, parents).astype(jnp.float32).astype(jnp.bfloat16)
        pid_slots = jnp.dot(pick, pid, preferred_element_type=jnp.float32)
        for d in range(n_seq):
            slots[d, :, :LANES] = pid_slots[d * per_peer : (d + 1) * per_peer].astype(
                jnp.bfloat16
            )
        block_lanes = 4 * LANES
        for g in range(KV_HEADS):
            if g < len(load_q):
                load_q[g].wait()
            for c in range(group_width // block_lanes):
                first = g * group_width + c * block_lanes
                part = jnp.dot(
                    pick,
                    q_ref[:, :, first : first + block_lanes].reshape(tokens, block_lanes),
                    preferred_element_type=jnp.float32,
                )
                for d in range(n_seq):
                    slots[d, :, LANES + first : LANES + first + block_lanes] = part[
                        d * per_peer : (d + 1) * per_peer
                    ].astype(jnp.bfloat16)
            if g == 0:
                pl.semaphore_wait(barrier, n_seq)
            for step in range(n_seq - 1, 0, -1):
                slots_to(step, g).start()
        q_to_partner.start()
        arrived[pl.ds(me, 1)] = slots[pl.ds(me, 1)]

    @pl.when(on_prefill)
    def _():
        pl.semaphore_wait(barrier, 1)
        for part in load_q:
            part.wait()

    for table in tables[2:]:
        table.wait()
    lengths = [suffix_len[r] for r in range(requests)]
    lane_page = iota((1, key_count), 1) // PAGE
    group_row = jnp.zeros((1, key_count), jnp.int32)
    base_row = jnp.zeros((1, key_count), jnp.int32)
    suf_pages = suffix_pages.shape[0]
    par_pages = parent_pages.shape[1]
    for j in range(key_count // PAGE):
        page = jnp.where(
            on_prefill,
            suffix_pages[j % suf_pages, j // suf_pages],
            parent_pages[j // par_pages, j % par_pages],
        )
        here = lane_page == page
        group_row = jnp.where(here, jnp.where(on_prefill, j // suf_pages, j // par_pages), group_row)
        base_row = jnp.where(
            here, jnp.where(on_prefill, j % suf_pages, j % par_pages) * PAGE, base_row
        )
    pos_row = base_row + (iota((1, key_count), 1) & (PAGE - 1))
    key_meta[0:1, :] = group_row
    key_meta[1:2, :] = pos_row

    load_step.wait()

    @pl.when(on_prefill)
    def _():
        for c in range(step_ref.shape[1] // (4 * LANES)):
            lanes = slice(c * 4 * LANES, (c + 1) * 4 * LANES)
            step_ref[:, lanes] = step_in[:, :, lanes].reshape(tokens, 4 * LANES)

    cuts = [parent_len[a] for a in range(parent_len.shape[0])]
    load_kv.wait()

    def bias_of(group, limit):
        keep = (key_meta[0:1, :] == group) & (key_meta[1:2, :] < limit)
        return jnp.where(keep, 0.0, MASKED_SCORE)

    def attend(g, query, bias, step_bias=None):
        rows = bias.shape[0]
        ks = slice(g * HEAD_DIM, (g + 1) * HEAD_DIM)
        vs = slice(key_width + g * HEAD_DIM, key_width + (g + 1) * HEAD_DIM)
        contract = (((1,), (1,)), ((), ()))

        def scores(keys, add):
            found = lax.dot_general(query, keys, contract, preferred_element_type=jnp.float32)
            return found.reshape(GROUP, rows, keys.shape[0]) * scale + add[None]

        def blend(term, values):
            term = term.reshape(GROUP * rows, values.shape[0]).astype(jnp.bfloat16)
            mixed = jnp.dot(term, values, preferred_element_type=jnp.float32)
            return mixed.reshape(GROUP, rows, HEAD_DIM)

        score = scores(kv_ref[:, ks], bias)
        top = jnp.max(score, axis=2, keepdims=True)
        if step_bias is not None:
            step_score = scores(step_ref[:, ks], step_bias)
            top = jnp.maximum(top, jnp.max(step_score, axis=2, keepdims=True))
        term = jnp.exp(score - top)
        total = jnp.sum(term, axis=2, keepdims=True)
        mixed = blend(term, kv_ref[:, vs])
        if step_bias is not None:
            step_term = jnp.exp(step_score - top)
            total = total + jnp.sum(step_term, axis=2, keepdims=True)
            mixed = mixed + blend(step_term, step_ref[:, vs])
        return mixed / total, top, total

    def record(g, top, total):
        lane = iota((top.shape[1], LANES), 1)
        stat = jnp.zeros(lane.shape, jnp.float32)
        for h in range(GROUP):
            stat = jnp.where(lane == g * GROUP + h, top[h], stat)
            stat = jnp.where(lane == half + g * GROUP + h, total[h], stat)
        return stat

    def log_sum(stat):
        lane = iota(stat.shape, 1)
        total = jnp.where(lane < heads_all, pltpu.roll(stat, half, 1), 1.0)
        return jnp.where(lane < heads_all, stat, 0.0) + jnp.log(total)

    @pl.when(on_prefill)
    def _():
        row = iota((tokens, 1), 0)
        request = row >> 1
        turn = row & 1
        length = spread(request, lengths)

        def lanes_of(head):
            return slice(head * HEAD_DIM, (head + 1) * HEAD_DIM)

        def own(head):
            return q_ref[:, :, lanes_of(head)].reshape(tokens, HEAD_DIM)

        def passed(head):
            return partner_q[:, :, lanes_of(head)].reshape(tokens, HEAD_DIM)

        def serve(head, value):
            out_ref[:, lanes_of(head)] = value.astype(jnp.bfloat16)

        def keep(head, value):
            near_send[:, lanes_of(head)] = value

        q_to_partner.wait_recv()
        bias = bias_of(request, length)
        step_key = iota((tokens, tokens), 1)
        step_keep = ((step_key >> 1) == request) & ((step_key & 1) < turn + 1)
        step_bias = jnp.where(step_keep, 0.0, MASKED_SCORE)
        stat = jnp.zeros((tokens, LANES), jnp.float32)
        for g in range(KV_HEADS):
            heads = range(g * GROUP, (g + 1) * GROUP)
            query = jnp.concatenate([passed(head) for head in heads], axis=0)
            mixed, top, total = attend(g, query, bias, step_bias)
            for h, head in enumerate(heads):
                keep(head, mixed[h])
            stat = stat + record(g, top, total)
        near_send[:, q_width:] = log_sum(stat)
        o_to_partner.start()
        bias = bias_of(request, length - 1 + turn)
        for g in range(KV_HEADS):
            heads = range(g * GROUP, (g + 1) * GROUP)
            query = jnp.concatenate([own(head) for head in heads], axis=0)
            mixed, _, _ = attend(g, query, bias)
            for h, head in enumerate(heads):
                serve(head, mixed[h])
        o_to_partner.wait_send()

    def answer(first, count, g, mine):
        peers = [first + i for i in range(count)]
        rows = pl.ds(first * per_peer, count * per_peer)
        slots_from(first // quad, g, quad - 1 if mine else quad).wait_recv()

        def gathered(first):
            return jnp.concatenate(
                [
                    arrived[peer, :, first : first + LANES].astype(jnp.float32) for peer in peers
                ],
                axis=0,
            )

        if g == 0:
            group = gathered(0).astype(jnp.int32)[:, 0:1]
            slot_bias[rows, :] = bias_of(group, spread(group, cuts))
        query = jnp.concatenate(
            [
                gathered(LANES + head * HEAD_DIM).astype(jnp.bfloat16)
                for head in range(g * GROUP, (g + 1) * GROUP)
            ],
            axis=0,
        )
        mixed, top, total = attend(g, query, slot_bias[rows, :])
        for h in range(GROUP):
            head = g * GROUP + h
            for i, peer in enumerate(peers):
                ret_send[peer, :, head * HEAD_DIM : (head + 1) * HEAD_DIM] = mixed[
                    h, i * per_peer : (i + 1) * per_peer
                ].astype(jnp.bfloat16)
        stat = record(g, top, total)
        if g > 0:
            stat = stat + slot_stat[rows, :]
        if g < KV_HEADS - 1:
            slot_stat[rows, :] = stat
        else:
            value = log_sum(stat)
            high = value.astype(jnp.bfloat16).astype(jnp.float32)
            rest = value - high
            middle = rest.astype(jnp.bfloat16).astype(jnp.float32)
            low = rest - middle
            lane = iota(value.shape, 1)
            packed = jnp.where(
                lane < heads_all,
                high,
                jnp.where(
                    lane < 2 * heads_all,
                    pltpu.roll(middle, heads_all, 1),
                    pltpu.roll(low, 2 * heads_all, 1),
                ),
            )
            for i, peer in enumerate(peers):
                ret_send[peer, :, q_width:] = packed[
                    i * per_peer : (i + 1) * per_peer
                ].astype(jnp.bfloat16)

        for peer in peers:
            if mine:
                pl.when(peer != me)(lambda: out_to(peer, g).start())
            else:
                out_to(peer, g).start()

    @pl.when(on_decode)
    def _():
        if n_seq == 2 * quad == 8:
            upper = me // quad
            for g in range(KV_HEADS):
                answer(quad - quad * upper, quad, g, False)
                answer(my_quad, quad, g, True)
        else:
            for g in range(KV_HEADS):
                answer(my_quad, quad, g, True)
                each(
                    1,
                    n_seq // quad,
                    lambda i: answer(lax.rem(my_quad + i * quad, n_seq), quad, g, False),
                )

    @pl.when(on_decode)
    def _():
        ret[pl.ds(me, 1)] = ret_send[pl.ds(me, 1)]
        tok = iota((tokens, 1), 0)
        target = 2 * spread(tok >> 1, places) + (tok & 1)
        unpick = jnp.where(iota((tokens, slot_rows), 1) == target, 1.0, 0.0)
        o_to_partner.wait_recv()
        pick_back = unpick.astype(jnp.bfloat16)

        def came(first):
            rows = jnp.concatenate(
                [ret[s, :, first : first + LANES].astype(jnp.float32) for s in range(n_seq)],
                axis=0,
            ).astype(jnp.bfloat16)
            return jnp.dot(pick_back, rows, preferred_element_type=jnp.float32)

        last = KV_HEADS - 1
        for g in range(last):
            out_from(g).wait_recv()
            for head in range(g * GROUP, (g + 1) * GROUP):
                far_out[:, head * HEAD_DIM : (head + 1) * HEAD_DIM] = came(head * HEAD_DIM)
        out_from(last).wait_recv()
        parts = came(q_width)
        far = (
            parts
            + pltpu.roll(parts, LANES - heads_all, 1)
            + pltpu.roll(parts, LANES - 2 * heads_all, 1)
        )
        near = partner_o[:, q_width:]
        top = jnp.maximum(far, near)
        far_weight = jnp.exp(far - top)
        far_share = far_weight / (far_weight + jnp.exp(near - top))
        for head in range(heads_all):
            part = slice(head * HEAD_DIM, (head + 1) * HEAD_DIM)
            close = partner_o[:, part]
            distant = came(head * HEAD_DIM) if head // GROUP == last else far_out[:, part]
            out_ref[:, part] = (
                close + (distant - close) * far_share[:, head : head + 1]
            ).astype(jnp.bfloat16)
        q_to_partner.wait_send()
        rows = pl.ds(0, n_seq - 1)
        remote(
            slots.at[rows], arrived.at[rows], send_sem.at[0], recv_sem.at[0, 0], {"seq": me}
        ).wait_send()
        remote(
            ret_send.at[rows], ret.at[rows], send_sem.at[1], orecv_sem.at[0], {"seq": me}
        ).wait_send()


def local(
    kv_store, queries, step_kv, suffix_pages, suffix_len, owner, parent_id, parent_pages, parent_len
):
    n_seq = lax.axis_size("seq")
    page_store = kv_store[0]
    requests, turns, q_width = queries.shape[1:]
    tokens = requests * turns
    cap = max(4, 2 * requests // n_seq)
    per_peer = 2 * cap
    bf16, f32 = jnp.bfloat16, jnp.float32
    vmem = pl.BlockSpec(memory_space=pltpu.VMEM)
    hbm = pl.BlockSpec(memory_space=pl.ANY)
    dma = pltpu.SemaphoreType.DMA
    served = pl.pallas_call(
        functools.partial(kernel, n_seq, cap),
        out_shape=pltpu.VMEM((tokens, q_width), bf16),
        in_specs=[hbm] * 9,
        out_specs=vmem,
        scratch_shapes=[
            pltpu.SMEM((requests,), jnp.int32),
            pltpu.SMEM((requests,), jnp.int32),
            pltpu.SMEM((requests,), jnp.int32),
            pltpu.SMEM(suffix_pages.shape[::-1], jnp.int32),
            pltpu.SMEM(parent_pages.shape, jnp.int32),
            pltpu.SMEM(parent_len.shape, jnp.int32),
            pltpu.VMEM((requests, turns, q_width), bf16),
            pltpu.VMEM(page_store.shape, bf16),
            pltpu.VMEM(step_kv.shape, bf16),
            pltpu.VMEM((tokens, step_kv.shape[2]), bf16),
            pltpu.VMEM((n_seq, per_peer, q_width + LANES), bf16),
            pltpu.VMEM((n_seq, per_peer, q_width + LANES), bf16),
            pltpu.VMEM((8, page_store.shape[0]), jnp.int32),
            pltpu.VMEM((n_seq * per_peer, page_store.shape[0]), f32),
            pltpu.VMEM((n_seq * per_peer, LANES), f32),
            pltpu.VMEM((tokens, q_width), f32),
            pltpu.VMEM((tokens, q_width + LANES), f32),
            pltpu.VMEM((n_seq, per_peer, q_width + LANES), bf16),
            pltpu.VMEM((n_seq, per_peer, q_width + LANES), bf16),
            pltpu.VMEM((requests, turns, q_width), bf16),
            pltpu.VMEM((tokens, q_width + LANES), f32),
            dma((10,)),
            dma((2,)),
            dma((n_seq // min(4, n_seq), KV_HEADS)),
            dma((KV_HEADS,)),
            dma((2,)),
            dma((2,)),
        ],
        compiler_params=pltpu.CompilerParams(
            collective_id=0, has_side_effects=True, vmem_limit_bytes=60 * 1024 * 1024
        ),
    )(
        owner.reshape(-1),
        parent_id,
        suffix_len,
        suffix_pages.T,
        parent_pages,
        parent_len,
        queries[0],
        page_store,
        step_kv,
    )
    return served.reshape(1, requests, turns, q_width)


def solution(mesh):
    in_specs = (
        P("role", ("groups", "seq"), None),
        P("role", ("groups", "seq"), None, None),
        P(("groups", "seq"), None, None),
        P(("groups", "seq"), None),
        P(("groups", "seq")),
        P(("groups", "seq"), None),
        P(("groups", "seq")),
        P(("groups", "seq"), None),
        P(("groups", "seq")),
    )
    out_specs = P("role", ("groups", "seq"), None, None)
    return jax.shard_map(local, mesh=mesh, in_specs=in_specs, out_specs=out_specs, check_vma=False)
```

```python
import functools

import jax
import jax.numpy as jnp
from jax import lax
from jax.experimental import pallas as pl
from jax.experimental.pallas import tpu as pltpu
from jax.sharding import PartitionSpec as P

HEAD_DIM = 128
KV_HEADS = 4
GROUP = 8
PAGE = 16
LANES = 128

MASKED_SCORE = -1e30
MESH = pl.DeviceIdType.MESH


def iota(shape, dim):
    return lax.broadcasted_iota(jnp.int32, shape, dim)


def spread(index, scalars):
    out = jnp.zeros(index.shape, jnp.int32)
    for i, scalar in enumerate(scalars):
        out = jnp.where(index == i, scalar, out)
    return out


def kernel(
    n_seq,
    cap,
    owner_hbm,
    parent_id_hbm,
    suffix_len_hbm,
    suffix_pages_hbm,
    parent_pages_hbm,
    parent_len_hbm,
    q_hbm,
    kv_hbm,
    step_hbm,
    out_ref,
    owner,
    parent_id,
    suffix_len,
    suffix_pages,
    parent_pages,
    parent_len,
    q_ref,
    kv_ref,
    step_in,
    step_ref,
    slots,
    arrived,
    key_meta,
    slot_bias,
    slot_stat,
    far_out,
    near_send,
    ret_send,
    ret,
    partner_q,
    partner_o,
    load_sem,
    send_sem,
    recv_sem,
    orecv_sem,
    psend_sem,
    precv_sem,
):
    role = lax.axis_index("role")
    me = lax.axis_index("seq")
    requests, turns, q_width = q_ref.shape
    tokens = requests * turns
    per_peer = 2 * cap
    slot_rows = n_seq * per_peer
    key_count = kv_ref.shape[0]
    key_width = KV_HEADS * HEAD_DIM
    scale = HEAD_DIM ** (-0.5)
    partner = {"role": 1 - role}
    on_decode = role == 1
    on_prefill = role == 0
    heads_all = KV_HEADS * GROUP
    group_width = GROUP * HEAD_DIM
    half = LANES // 2
    quad = min(4, n_seq)
    my_quad = me // quad * quad
    bits = [(me // 2**b) % 2 for b in range(n_seq.bit_length() - 1)]

    def peer_at(step):
        peer = me
        for b, mine in enumerate(bits):
            if isinstance(step, int):
                if (step >> b) & 1:
                    peer = peer + 2**b * (1 - 2 * mine)
            else:
                peer = peer + 2**b * (1 - 2 * mine) * ((step // 2**b) % 2)
        return peer

    def each(first, last, action):
        def body(i, carry):
            action(i)
            return carry

        lax.fori_loop(first, last, body, 0)

    barrier = pltpu.get_barrier_semaphore()

    def greet(peer):
        pl.semaphore_signal(barrier, inc=1, device_id={"seq": peer}, device_id_type=MESH)

    pl.semaphore_signal(barrier, inc=1, device_id=partner, device_id_type=MESH)

    @pl.when(on_decode)
    def _():
        for step in range(n_seq - 1, 0, -1):
            greet(peer_at(step))

    tables = [
        pltpu.make_async_copy(src, dst, load_sem.at[i])
        for i, (src, dst) in enumerate(
            (
                (owner_hbm, owner),
                (parent_id_hbm, parent_id),
                (suffix_len_hbm, suffix_len),
                (suffix_pages_hbm, suffix_pages),
                (parent_pages_hbm, parent_pages),
                (parent_len_hbm, parent_len),
            )
        )
    ]
    load_step = pltpu.make_async_copy(step_hbm, step_in, load_sem.at[6])
    load_kv = pltpu.make_async_copy(kv_hbm, kv_ref, load_sem.at[7])

    def out_lanes(g):
        return slice(g * group_width, (g + 1) * group_width)

    load_q = [
        pltpu.make_async_copy(
            q_hbm.at[:, :, lanes], q_ref.at[:, :, lanes], load_sem.at[8 + i]
        )
        for i, lanes in enumerate((slice(0, group_width), slice(group_width, q_width)))
    ]
    for table in tables[:2]:
        table.start()
    for part in load_q:
        part.start()
    for table in tables[2:]:
        table.start()
    load_kv.start()
    load_step.start()

    def remote(src, dst, ssem, rsem, device):
        return pltpu.make_async_remote_copy(
            src_ref=src,
            dst_ref=dst,
            send_sem=ssem,
            recv_sem=rsem,
            device_id=device,
            device_id_type=MESH,
        )

    q_to_partner = remote(q_ref, partner_q, psend_sem.at[0], precv_sem.at[0], partner)
    o_to_partner = remote(near_send, partner_o, psend_sem.at[1], precv_sem.at[1], partner)

    def q_lanes(g):
        first = 0 if g == 0 else LANES + g * group_width
        return slice(first, LANES + (g + 1) * group_width)

    def ret_lanes(g):
        last = LANES if g == KV_HEADS - 1 else 0
        return slice(g * group_width, (g + 1) * group_width + last)

    def slots_to(step, g):
        peer = peer_at(step)
        return remote(
            slots.at[peer, :, q_lanes(g)],
            arrived.at[me, :, q_lanes(g)],
            send_sem.at[0],
            recv_sem.at[me // quad, g],
            {"seq": peer},
        )

    def slots_from(u, g, count):
        rows = pl.ds(0, count)
        return remote(
            slots.at[rows, :, q_lanes(g)],
            arrived.at[rows, :, q_lanes(g)],
            send_sem.at[0],
            recv_sem.at[u, g],
            {"seq": me},
        )

    def out_to(peer, g):
        return remote(
            ret_send.at[peer, :, ret_lanes(g)],
            ret.at[me, :, ret_lanes(g)],
            send_sem.at[1],
            orecv_sem.at[g],
            {"seq": peer},
        )

    def out_from(g):
        rows = pl.ds(0, n_seq - 1)
        return remote(
            ret_send.at[rows, :, ret_lanes(g)],
            ret.at[rows, :, ret_lanes(g)],
            send_sem.at[1],
            orecv_sem.at[g],
            {"seq": me},
        )

    for table in tables[:2]:
        table.wait()
    owners = [owner[r] for r in range(requests)]
    places = []
    for r in range(requests):
        rank = jnp.int32(0)
        for e in range(r):
            rank = rank + jnp.where(owners[e] == owners[r], 1, 0)
        places.append(owners[r] * cap + rank)
    parents = [parent_id[r] for r in range(requests)]

    @pl.when(on_decode)
    def _():
        col = iota((1, tokens), 1)
        target = 2 * spread(col >> 1, places) + (col & 1)
        pick = jnp.where(iota((slot_rows, tokens), 0) == target, 1.0, 0.0).astype(jnp.bfloat16)
        tok = iota((tokens, LANES), 0) >> 1
        pid = spread(tok, parents).astype(jnp.float32).astype(jnp.bfloat16)
        pid_slots = jnp.dot(pick, pid, preferred_element_type=jnp.float32)
        for d in range(n_seq):
            slots[d, :, :LANES] = pid_slots[d * per_peer : (d + 1) * per_peer].astype(
                jnp.bfloat16
            )
        block_lanes = 4 * LANES
        for g in range(KV_HEADS):
            if g < len(load_q):
                load_q[g].wait()
            for c in range(group_width // block_lanes):
                first = g * group_width + c * block_lanes
                part = jnp.dot(
                    pick,
                    q_ref[:, :, first : first + block_lanes].reshape(tokens, block_lanes),
                    preferred_element_type=jnp.float32,
                )
                for d in range(n_seq):
                    slots[d, :, LANES + first : LANES + first + block_lanes] = part[
                        d * per_peer : (d + 1) * per_peer
                    ].astype(jnp.bfloat16)
            if g == 0:
                pl.semaphore_wait(barrier, n_seq)
            for step in range(n_seq - 1, 0, -1):
                slots_to(step, g).start()
        q_to_partner.start()
        arrived[pl.ds(me, 1)] = slots[pl.ds(me, 1)]

    @pl.when(on_prefill)
    def _():
        pl.semaphore_wait(barrier, 1)
        for part in load_q:
            part.wait()

    for table in tables[2:]:
        table.wait()
    lengths = [suffix_len[r] for r in range(requests)]
    lane_page = iota((1, key_count), 1) // PAGE
    group_row = jnp.zeros((1, key_count), jnp.int32)
    base_row = jnp.zeros((1, key_count), jnp.int32)
    suf_pages = suffix_pages.shape[0]
    par_pages = parent_pages.shape[1]
    for j in range(key_count // PAGE):
        page = jnp.where(
            on_prefill,
            suffix_pages[j % suf_pages, j // suf_pages],
            parent_pages[j // par_pages, j % par_pages],
        )
        here = lane_page == page
        group_row = jnp.where(here, jnp.where(on_prefill, j // suf_pages, j // par_pages), group_row)
        base_row = jnp.where(
            here, jnp.where(on_prefill, j % suf_pages, j % par_pages) * PAGE, base_row
        )
    pos_row = base_row + (iota((1, key_count), 1) & (PAGE - 1))
    key_meta[0:1, :] = group_row
    key_meta[1:2, :] = pos_row

    load_step.wait()

    @pl.when(on_prefill)
    def _():
        for c in range(step_ref.shape[1] // (4 * LANES)):
            lanes = slice(c * 4 * LANES, (c + 1) * 4 * LANES)
            step_ref[:, lanes] = step_in[:, :, lanes].reshape(tokens, 4 * LANES)

    cuts = [parent_len[a] for a in range(parent_len.shape[0])]
    load_kv.wait()

    def bias_of(group, limit):
        keep = (key_meta[0:1, :] == group) & (key_meta[1:2, :] < limit)
        return jnp.where(keep, 0.0, MASKED_SCORE)

    def attend(g, query, bias, step_bias=None):
        rows = bias.shape[0]
        ks = slice(g * HEAD_DIM, (g + 1) * HEAD_DIM)
        vs = slice(key_width + g * HEAD_DIM, key_width + (g + 1) * HEAD_DIM)
        contract = (((1,), (1,)), ((), ()))

        def scores(keys, add):
            found = lax.dot_general(query, keys, contract, preferred_element_type=jnp.float32)
            return found.reshape(GROUP, rows, keys.shape[0]) * scale + add[None]

        def blend(term, values):
            term = term.reshape(GROUP * rows, values.shape[0]).astype(jnp.bfloat16)
            mixed = jnp.dot(term, values, preferred_element_type=jnp.float32)
            return mixed.reshape(GROUP, rows, HEAD_DIM)

        score = scores(kv_ref[:, ks], bias)
        top = jnp.max(score, axis=2, keepdims=True)
        if step_bias is not None:
            step_score = scores(step_ref[:, ks], step_bias)
            top = jnp.maximum(top, jnp.max(step_score, axis=2, keepdims=True))
        term = jnp.exp(score - top)
        total = jnp.sum(term, axis=2, keepdims=True)
        mixed = blend(term, kv_ref[:, vs])
        if step_bias is not None:
            step_term = jnp.exp(step_score - top)
            total = total + jnp.sum(step_term, axis=2, keepdims=True)
            mixed = mixed + blend(step_term, step_ref[:, vs])
        return mixed / total, top, total

    def record(g, top, total):
        lane = iota((top.shape[1], LANES), 1)
        stat = jnp.zeros(lane.shape, jnp.float32)
        for h in range(GROUP):
            stat = jnp.where(lane == g * GROUP + h, top[h], stat)
            stat = jnp.where(lane == half + g * GROUP + h, total[h], stat)
        return stat

    def log_sum(stat):
        lane = iota(stat.shape, 1)
        total = jnp.where(lane < heads_all, pltpu.roll(stat, half, 1), 1.0)
        return jnp.where(lane < heads_all, stat, 0.0) + jnp.log(total)

    @pl.when(on_prefill)
    def _():
        row = iota((tokens, 1), 0)
        request = row >> 1
        turn = row & 1
        length = spread(request, lengths)

        def lanes_of(head):
            return slice(head * HEAD_DIM, (head + 1) * HEAD_DIM)

        def own(head):
            return q_ref[:, :, lanes_of(head)].reshape(tokens, HEAD_DIM)

        def passed(head):
            return partner_q[:, :, lanes_of(head)].reshape(tokens, HEAD_DIM)

        def serve(head, value):
            out_ref[:, lanes_of(head)] = value.astype(jnp.bfloat16)

        def keep(head, value):
            near_send[:, lanes_of(head)] = value

        q_to_partner.wait_recv()
        bias = bias_of(request, length)
        step_key = iota((tokens, tokens), 1)
        step_keep = ((step_key >> 1) == request) & ((step_key & 1) < turn + 1)
        step_bias = jnp.where(step_keep, 0.0, MASKED_SCORE)
        stat = jnp.zeros((tokens, LANES), jnp.float32)
        for g in range(KV_HEADS):
            heads = range(g * GROUP, (g + 1) * GROUP)
            query = jnp.concatenate([passed(head) for head in heads], axis=0)
            mixed, top, total = attend(g, query, bias, step_bias)
            for h, head in enumerate(heads):
                keep(head, mixed[h])
            stat = stat + record(g, top, total)
        near_send[:, q_width:] = log_sum(stat)
        o_to_partner.start()
        bias = bias_of(request, length - 1 + turn)
        for g in range(KV_HEADS):
            heads = range(g * GROUP, (g + 1) * GROUP)
            query = jnp.concatenate([own(head) for head in heads], axis=0)
            mixed, _, _ = attend(g, query, bias)
            for h, head in enumerate(heads):
                serve(head, mixed[h])
        o_to_partner.wait_send()

    def answer(first, count, g, mine):
        peers = [first + i for i in range(count)]
        rows = pl.ds(first * per_peer, count * per_peer)
        slots_from(first // quad, g, quad - 1 if mine else quad).wait_recv()

        def gathered(first):
            return jnp.concatenate(
                [
                    arrived[peer, :, first : first + LANES].astype(jnp.float32) for peer in peers
                ],
                axis=0,
            )

        if g == 0:
            group = gathered(0).astype(jnp.int32)[:, 0:1]
            slot_bias[rows, :] = bias_of(group, spread(group, cuts))
        query = jnp.concatenate(
            [
                gathered(LANES + head * HEAD_DIM).astype(jnp.bfloat16)
                for head in range(g * GROUP, (g + 1) * GROUP)
            ],
            axis=0,
        )
        mixed, top, total = attend(g, query, slot_bias[rows, :])
        for h in range(GROUP):
            head = g * GROUP + h
            for i, peer in enumerate(peers):
                ret_send[peer, :, head * HEAD_DIM : (head + 1) * HEAD_DIM] = mixed[
                    h, i * per_peer : (i + 1) * per_peer
                ].astype(jnp.bfloat16)
        stat = record(g, top, total)
        if g > 0:
            stat = stat + slot_stat[rows, :]
        if g < KV_HEADS - 1:
            slot_stat[rows, :] = stat
        else:
            value = log_sum(stat)
            high = value.astype(jnp.bfloat16).astype(jnp.float32)
            rest = value - high
            middle = rest.astype(jnp.bfloat16).astype(jnp.float32)
            low = rest - middle
            lane = iota(value.shape, 1)
            packed = jnp.where(
                lane < heads_all,
                high,
                jnp.where(
                    lane < 2 * heads_all,
                    pltpu.roll(middle, heads_all, 1),
                    pltpu.roll(low, 2 * heads_all, 1),
                ),
            )
            for i, peer in enumerate(peers):
                ret_send[peer, :, q_width:] = packed[
                    i * per_peer : (i + 1) * per_peer
                ].astype(jnp.bfloat16)

        if mine:
            for step in range(quad - 1, 0, -1):
                out_to(peer_at(step), g).start()
        else:
            for peer in peers:
                out_to(peer, g).start()

    @pl.when(on_decode)
    def _():
        if n_seq == 2 * quad == 8:
            upper = me // quad
            for g in range(KV_HEADS):
                answer(quad - quad * upper, quad, g, False)
                answer(my_quad, quad, g, True)
        else:
            for g in range(KV_HEADS):
                answer(my_quad, quad, g, True)
                each(
                    1,
                    n_seq // quad,
                    lambda i: answer(lax.rem(my_quad + i * quad, n_seq), quad, g, False),
                )

    @pl.when(on_decode)
    def _():
        ret[pl.ds(me, 1)] = ret_send[pl.ds(me, 1)]
        tok = iota((tokens, 1), 0)
        target = 2 * spread(tok >> 1, places) + (tok & 1)
        unpick = jnp.where(iota((tokens, slot_rows), 1) == target, 1.0, 0.0)
        o_to_partner.wait_recv()
        pick_back = unpick.astype(jnp.bfloat16)

        def came(first):
            rows = jnp.concatenate(
                [ret[s, :, first : first + LANES].astype(jnp.float32) for s in range(n_seq)],
                axis=0,
            ).astype(jnp.bfloat16)
            return jnp.dot(pick_back, rows, preferred_element_type=jnp.float32)

        last = KV_HEADS - 1
        for g in range(last):
            out_from(g).wait_recv()
            for head in range(g * GROUP, (g + 1) * GROUP):
                far_out[:, head * HEAD_DIM : (head + 1) * HEAD_DIM] = came(head * HEAD_DIM)
        out_from(last).wait_recv()
        parts = came(q_width)
        far = (
            parts
            + pltpu.roll(parts, LANES - heads_all, 1)
            + pltpu.roll(parts, LANES - 2 * heads_all, 1)
        )
        near = partner_o[:, q_width:]
        top = jnp.maximum(far, near)
        far_weight = jnp.exp(far - top)
        far_share = far_weight / (far_weight + jnp.exp(near - top))
        for head in range(heads_all):
            part = slice(head * HEAD_DIM, (head + 1) * HEAD_DIM)
            close = partner_o[:, part]
            distant = came(head * HEAD_DIM) if head // GROUP == last else far_out[:, part]
            out_ref[:, part] = (
                close + (distant - close) * far_share[:, head : head + 1]
            ).astype(jnp.bfloat16)
        q_to_partner.wait_send()
        rows = pl.ds(0, n_seq - 1)
        remote(
            slots.at[rows], arrived.at[rows], send_sem.at[0], recv_sem.at[0, 0], {"seq": me}
        ).wait_send()
        remote(
            ret_send.at[rows], ret.at[rows], send_sem.at[1], orecv_sem.at[0], {"seq": me}
        ).wait_send()


def local(
    kv_store, queries, step_kv, suffix_pages, suffix_len, owner, parent_id, parent_pages, parent_len
):
    n_seq = lax.axis_size("seq")
    page_store = kv_store[0]
    requests, turns, q_width = queries.shape[1:]
    tokens = requests * turns
    cap = max(4, 2 * requests // n_seq)
    per_peer = 2 * cap
    bf16, f32 = jnp.bfloat16, jnp.float32
    vmem = pl.BlockSpec(memory_space=pltpu.VMEM)
    hbm = pl.BlockSpec(memory_space=pl.ANY)
    dma = pltpu.SemaphoreType.DMA
    served = pl.pallas_call(
        functools.partial(kernel, n_seq, cap),
        out_shape=pltpu.VMEM((tokens, q_width), bf16),
        in_specs=[hbm] * 9,
        out_specs=vmem,
        scratch_shapes=[
            pltpu.SMEM((requests,), jnp.int32),
            pltpu.SMEM((requests,), jnp.int32),
            pltpu.SMEM((requests,), jnp.int32),
            pltpu.SMEM(suffix_pages.shape[::-1], jnp.int32),
            pltpu.SMEM(parent_pages.shape, jnp.int32),
            pltpu.SMEM(parent_len.shape, jnp.int32),
            pltpu.VMEM((requests, turns, q_width), bf16),
            pltpu.VMEM(page_store.shape, bf16),
            pltpu.VMEM(step_kv.shape, bf16),
            pltpu.VMEM((tokens, step_kv.shape[2]), bf16),
            pltpu.VMEM((n_seq, per_peer, q_width + LANES), bf16),
            pltpu.VMEM((n_seq, per_peer, q_width + LANES), bf16),
            pltpu.VMEM((8, page_store.shape[0]), jnp.int32),
            pltpu.VMEM((n_seq * per_peer, page_store.shape[0]), f32),
            pltpu.VMEM((n_seq * per_peer, LANES), f32),
            pltpu.VMEM((tokens, q_width), f32),
            pltpu.VMEM((tokens, q_width + LANES), f32),
            pltpu.VMEM((n_seq, per_peer, q_width + LANES), bf16),
            pltpu.VMEM((n_seq, per_peer, q_width + LANES), bf16),
            pltpu.VMEM((requests, turns, q_width), bf16),
            pltpu.VMEM((tokens, q_width + LANES), f32),
            dma((10,)),
            dma((2,)),
            dma((n_seq // min(4, n_seq), KV_HEADS)),
            dma((KV_HEADS,)),
            dma((2,)),
            dma((2,)),
        ],
        compiler_params=pltpu.CompilerParams(
            collective_id=0, has_side_effects=True, vmem_limit_bytes=60 * 1024 * 1024
        ),
    )(
        owner.reshape(-1),
        parent_id,
        suffix_len,
        suffix_pages.T,
        parent_pages,
        parent_len,
        queries[0],
        page_store,
        step_kv,
    )
    return served.reshape(1, requests, turns, q_width)


def solution(mesh):
    in_specs = (
        P("role", ("groups", "seq"), None),
        P("role", ("groups", "seq"), None, None),
        P(("groups", "seq"), None, None),
        P(("groups", "seq"), None),
        P(("groups", "seq")),
        P(("groups", "seq"), None),
        P(("groups", "seq")),
        P(("groups", "seq"), None),
        P(("groups", "seq")),
    )
    out_specs = P("role", ("groups", "seq"), None, None)
    return jax.shard_map(local, mesh=mesh, in_specs=in_specs, out_specs=out_specs, check_vma=False)
```
